32 devices in a mesh: px: 16 (over z, y, core), py: 2 (over x).
Axes of the slice: x: 2, y: 2, z: 4, core: 2. Of those that a mesh axis runs over, the one named last changes fastest.
Arguments:
- spectrum: float32 [2, 3, 128, 128, 512], P(None, None, 'px', 'py'), may hold values from -3 to 3
- scalar: float32 [1024, 256, 256], P('px', 'py'), may hold values from -6 to 6
Outputs:
- tendency: float32 [2, 3, 128, 128, 512], P(None, None, 'px', 'py')
- advanced: float32 [1024, 256, 256], P('px', 'py')
The draws below stay inside these ranges and needn't reach their ends.
All inputs are finite; a program needn't handle non-finite values.
Results may differ from the reference program's by a relative error of at most 0.0003.
Values sent between devices are 32-bit elements; how exact they have to be, the bound alone decides.
A program may use at most 320 MiB of HBM per device.

```python
import math
import jax
import jax.numpy as jnp

V1 = 512
V2 = 128
V3 = 128
NSUB = 3


def shard_levels(own_key, extent, shards, low, top_value):
    gain = 1.0
    for dim, shards_of in shards:
        draws = jax.random.uniform(jax.random.fold_in(jax.random.fold_in(own_key, 6), dim), (shards_of,), jnp.float32, low / len(shards), top_value / len(shards))
        gain = gain * jnp.repeat(jnp.exp(draws), extent[dim] // shards_of).reshape((-1,) + (1,) * (len(extent) - 1 - dim))
    return gain


def gaussian(stream_key, shape, scale, most, split=(), held_as=jnp.bfloat16):
    drawn = jax.random.normal(stream_key, shape, jnp.float32) * scale
    if len(split) > 0:
        drawn = shard_levels(stream_key, shape, split, -0.22, 0.18) * drawn
    return jnp.clip(drawn, min=-most, max=most).astype(held_as)


def setup_inputs(seed: int = 0) -> dict:
    key_of = jax.random.split(jax.random.key(seed), 3)
    return {
        "spectrum": gaussian(key_of[0], (2, 3, V2, V3, V1), 0.5, 3.0, ((2, 16), (3, 2)), jnp.float32),
        "scalar": gaussian(key_of[1], (2 * V1, 2 * V2, 2 * V3), 1.0, 6.0, ((0, 16), (1, 2)), jnp.float32),
    }


STEP_RATIO = 0.08
DIFFUSION_RATIO = 1.0


def wavenumbers(length):
    index = jnp.arange(length, dtype=jnp.int32)
    signed = jnp.where(index < length // 2, index, index - length)
    return (2.0 * math.pi / length) * signed.astype(jnp.float32)


def upsample(field, axis):
    middles = (9.0 * (field + jnp.roll(field, -1, axis)) - (jnp.roll(field, 1, axis) + jnp.roll(field, -2, axis))) / 16.0
    paired = jnp.stack([field, middles], axis=axis + 1)
    shape = list(field.shape)
    shape[axis] = 2 * shape[axis]
    return paired.reshape(shape)


def limited_slope(first, second):
    return 0.5 * (jnp.sign(first) + jnp.sign(second)) * jnp.minimum(jnp.abs(first), jnp.abs(second))


def spin_divergence(theta, speed, axis):
    ahead = jnp.roll(theta, -1, axis)
    jump = ahead - theta
    slope = limited_slope(jnp.roll(jump, 1, axis), jump)
    left = theta + 0.5 * slope
    right = ahead - 0.5 * jnp.roll(slope, -1, axis)
    face = 0.5 * (speed + jnp.roll(speed, -1, axis))
    flux = jnp.maximum(face, 0.0) * left + jnp.minimum(face, 0.0) * right - DIFFUSION_RATIO * jump
    return flux - jnp.roll(flux, 1, axis)


def reference(spectrum, scalar):
    coeffs = jnp.transpose(spectrum[0] + 1j * spectrum[1], (0, 3, 1, 2))
    wave_first = wavenumbers(V1)[:, None, None]
    wave_second = wavenumbers(V2)[None, :, None]
    wave_third = wavenumbers(V3)[None, None, :]
    cross = jnp.stack([wave_second * coeffs[2] - wave_third * coeffs[1],
                       wave_third * coeffs[0] - wave_first * coeffs[2],
                       wave_first * coeffs[1] - wave_second * coeffs[0]])
    fields = jnp.concatenate([coeffs, 1j * cross])
    physical = jnp.real(jnp.fft.ifftn(fields, axes=(1, 2, 3), norm="ortho"))
    velocity = physical[:3]
    vorticity = physical[3:]
    speed = velocity
    for axis in (3, 1, 2):
        speed = upsample(speed, axis)
    theta = scalar
    for turn in range(NSUB):
        total = spin_divergence(theta, speed[0], 0) + spin_divergence(theta, speed[1], 1) + spin_divergence(theta, speed[2], 2)
        theta = theta - STEP_RATIO * total
    buoyancy = theta.reshape(V1, 2, V2, 2, V3, 2).mean(axis=(1, 3, 5))
    forcing = jnp.stack([velocity[1] * vorticity[2] - velocity[2] * vorticity[1],
                         velocity[2] * vorticity[0] - velocity[0] * vorticity[2],
                         velocity[0] * vorticity[1] - velocity[1] * vorticity[0] + buoyancy])
    spectral = jnp.transpose(jnp.fft.fftn(forcing, axes=(1, 2, 3), norm="ortho"), (0, 2, 3, 1))
    tendency = jnp.stack([jnp.real(spectral), jnp.imag(spectral)])
    return tendency, theta
```

```python
import math

import jax
import jax.numpy as jnp
from jax import lax
from jax.experimental import pallas as pl
from jax.experimental.pallas import tpu as pltpu
from jax.sharding import PartitionSpec as P

NSUB = 3


STEP_RATIO = 0.08
DIFFUSION_RATIO = 1.0


def padded(block, sides):
    for axis, dim, width in sides:
        count = lax.axis_size(axis)
        forward = [(i, i + 1) for i in range(count - 1)]
        forward.append((count - 1, 0))
        backward = [(target, source) for source, target in forward]
        low = lax.ppermute(
            lax.slice_in_dim(block, block.shape[dim] - width, None, axis=dim), axis, forward
        )
        high = lax.ppermute(lax.slice_in_dim(block, 0, width, axis=dim), axis, backward)
        block = jnp.concatenate([low, block, high], axis=dim)
    return block


def contract(form, left, right):
    return jnp.einsum(form, left, right, precision=lax.Precision.HIGH)


def dft_table(length, sign):
    index = jnp.arange(length, dtype=jnp.int32)
    product = index[:, None] * index[None, :] % length
    angle = 2.0 * math.pi / length * product.astype(jnp.float32)
    return (jnp.cos(angle), sign * jnp.sin(angle))


def complex_apply(real, imag, cosine, sine, form):
    return (
        contract(form, real, cosine) - contract(form, imag, sine),
        contract(form, real, sine) + contract(form, imag, cosine),
    )


def upsample_table(length):
    rows = jnp.arange(length, dtype=jnp.int32)[:, None]
    cols = jnp.arange(2 * length, dtype=jnp.int32)[None, :]
    half = cols // 2
    is_odd = cols % 2 == 1
    near = jnp.logical_or(rows == half, rows == (half + 1) % length)
    distant = jnp.logical_or(rows == (half - 1) % length, rows == (half + 2) % length)
    even_part = jnp.where(jnp.logical_and(jnp.logical_not(is_odd), rows == half), 1.0, 0.0)
    odd_part = jnp.where(
        is_odd, jnp.where(near, 9.0 / 16.0, 0.0) - jnp.where(distant, 1.0 / 16.0, 0.0), 0.0
    )
    return (even_part + odd_part).astype(jnp.float32)


def pair_table(length):
    rows = jnp.arange(2 * length, dtype=jnp.int32)[:, None]
    cols = jnp.arange(length, dtype=jnp.int32)[None, :]
    return jnp.where(rows // 2 == cols, 0.125, 0.0).astype(jnp.float32)


def wavenumbers(length):
    index = jnp.arange(length, dtype=jnp.int32)
    signed = jnp.where(index < length // 2, index, index - length)
    return 2.0 * math.pi / length * signed.astype(jnp.float32)


def across_px(pieces):
    return lax.all_to_all(pieces, "px", split_axis=2, concat_axis=1, tiled=True)


def across_py(pieces):
    return lax.all_to_all(pieces, "py", split_axis=2, concat_axis=1, tiled=True)


ROW_PAD = 8


def refine_rows(points):
    rows = jnp.arange(2 * points, dtype=jnp.int32)[:, None]
    cols = jnp.arange(points, dtype=jnp.int32)[None, :]

    def weights(row):
        half = row // 2
        gap = cols - half
        near = jnp.logical_or(gap == 0, gap == 1)
        distant = jnp.logical_or(gap == -1, gap == 2)
        odd = jnp.where(near, 9.0 / 16.0, 0.0) - jnp.where(distant, 1.0 / 16.0, 0.0)
        return jnp.where(row % 2 == 1, odd, jnp.where(gap == 0, 1.0, 0.0))

    cell = weights(rows)
    return cell, 0.5 * (cell + weights(rows + 1))


def split(value):
    high = value.astype(jnp.bfloat16)
    return high, (value - high.astype(jnp.float32)).astype(jnp.bfloat16)


def table_right(value, table):
    high, low = split(value)
    return jnp.dot(high, table, preferred_element_type=jnp.float32) + jnp.dot(
        low, table, preferred_element_type=jnp.float32
    )


def table_left(table, value):
    high, low = split(value)
    return jnp.dot(table, high, preferred_element_type=jnp.float32) + jnp.dot(
        table, low, preferred_element_type=jnp.float32
    )


def half_slope(first, second):
    low = jnp.minimum(first, second)
    high = jnp.maximum(first, second)
    return 0.5 * (jnp.maximum(low, 0.0) + jnp.minimum(high, 0.0))


def upwind(face, left, right, jump):
    return face * jnp.where(face > 0.0, left, right) - DIFFUSION_RATIO * jump


def line_div(theta, face, axis):
    size = theta.shape[axis]
    jump = pltpu.roll(theta, size - 1, axis) - theta
    slope = half_slope(pltpu.roll(jump, 1, axis), jump)
    right = pltpu.roll(theta - slope, size - 1, axis)
    flux = upwind(face, theta + slope, right, jump)
    return flux - pltpu.roll(flux, 1, axis)


def substep(prev, new, slope_ref, flux_ref, fx, fy, fz, store, first, count, chunk):
    def run(index, carry):
        row = pl.multiple_of(first + index * chunk, 8)
        here = pl.ds(row, chunk)
        inner = pl.ds(pl.multiple_of(row + ROW_PAD, 8), chunk)
        wide = pl.ds(row, chunk + 2 * ROW_PAD)
        b0 = prev[0, inner]
        b1 = prev[1, inner]
        a0 = new[0, inner]
        a1 = new[1, inner]
        jump_b = b1 - b0
        jump_m = a0 - b1
        slope_b = half_slope(jump_b, jump_m)
        slope_a = half_slope(jump_m, a1 - a0)
        flux_0 = upwind(fx[0, here], b0 + slope_ref[here], b1 - slope_b, jump_b)
        flux_1 = upwind(fx[1, here], b1 + slope_b, a0 - slope_a, jump_m)
        div_0 = flux_0 - flux_ref[here]
        div_1 = flux_1 - flux_0
        slope_ref[here] = slope_a
        flux_ref[here] = flux_1
        for plane, (base, div) in enumerate(((b0, div_0), (b1, div_1))):
            side = line_div(prev[plane, wide], fy[plane, wide], 0)
            side = side[ROW_PAD : ROW_PAD + chunk]
            total = div + side + line_div(base, fz[plane, here], 1)
            store(plane, row, base - STEP_RATIO * total)
        return carry

    lax.fori_loop(0, count, run, 0)


def march(
    theta_ref, speed_ref, my_ref, myf_ref, mz_ref, mzf_ref, py_ref, pz_ref,
    out_ref, pool_ref, t0, t1, t2, slopes, fluxes, fx, fy, fz,
):
    step = pl.program_id(0)
    now = lax.rem(step, 2)
    old = 1 - now
    rows = theta_ref.shape[1]
    inner = pl.ds(ROW_PAD, rows)
    t0[now, 0, inner] = theta_ref[0]
    t0[now, 1, inner] = theta_ref[1]
    slot = lax.rem(step, 3)
    before = lax.rem(step + 2, 3)
    oldest = lax.rem(step + 1, 3)
    for part in range(3):
        q0 = speed_ref[part, step]
        q1 = speed_ref[part, step + 1]
        qm = speed_ref[part, jnp.maximum(step - 1, 0)]
        q2 = speed_ref[part, step + 2]
        odd = (9.0 * (q0 + q1) - (qm + q2)) * (1.0 / 16.0)
        pair = (0.5 * (q0 + odd), 0.5 * (odd + q1)) if part == 0 else (q0, odd)
        for plane in range(2):
            line = table_right(pair[plane], (mzf_ref if part == 2 else mz_ref)[...])
            full = table_left((myf_ref if part == 1 else my_ref)[...], line)
            if part == 1:
                fy[slot, plane, inner] = full
            else:
                (fx if part == 0 else fz)[slot, plane] = full
    whole = rows // 24 if rows % 24 == 0 else rows // 8
    chunk = rows // whole

    def keep(target):
        def store(plane, row, value):
            target[now, plane, pl.ds(pl.multiple_of(row + ROW_PAD, 8), value.shape[0])] = value

        return store

    def emit(plane, row, value):
        out_ref[plane, pl.ds(pl.multiple_of(row - ROW_PAD, 8), value.shape[0])] = value

    substep(
        t0.at[old], t0.at[now], slopes.at[0], fluxes.at[0],
        fx.at[slot], fy.at[slot], fz.at[slot], keep(t1), 0, whole, chunk,
    )
    substep(
        t1.at[old], t1.at[now], slopes.at[1], fluxes.at[1],
        fx.at[before], fy.at[before], fz.at[before], keep(t2), 0, whole, chunk,
    )
    last = rows - 2 * ROW_PAD
    last_chunk = 32 if last % 32 == 0 else 8
    substep(
        t2.at[old], t2.at[now], slopes.at[2], fluxes.at[2],
        fx.at[oldest], fy.at[oldest], fz.at[oldest], emit, ROW_PAD, last // last_chunk, last_chunk,
    )
    both = out_ref[0] + out_ref[1]
    pool_ref[0] = table_left(py_ref[...], table_right(both, pz_ref[...]))


def scalar_steps(grown, widened):
    planes, rows, cells = grown.shape
    wide_first, wide_second, third = widened.shape[1:]
    steps = planes // 2
    first = planes - 12
    inner = rows - 2 * ROW_PAD
    cell, face = refine_rows(wide_second)
    up = upsample_table(third)
    up_face = 0.5 * (up + jnp.roll(up, -1, axis=1))
    pool_rows = (8.0 * pair_table(inner // 2)).T
    tables = [cell, face, up, up_face, pool_rows, pair_table(third)]
    tables = [table.astype(jnp.bfloat16) for table in tables]
    tall = rows + 2 * ROW_PAD
    f32 = jnp.float32
    return pl.pallas_call(
        march,
        grid=(steps,),
        in_specs=[
            pl.BlockSpec((2, rows, cells), lambda g: (g, 0, 0)),
            pl.BlockSpec((3, wide_first, wide_second, third), lambda g: (0, 0, 0, 0)),
        ]
        + [pl.BlockSpec(table.shape, lambda g: (0, 0)) for table in tables],
        out_specs=[
            pl.BlockSpec((2, inner, cells), lambda g: (jnp.maximum(g - 6, 0), 0, 0)),
            pl.BlockSpec((1, inner // 2, third), lambda g: (jnp.maximum(g - 6, 0), 0, 0)),
        ],
        out_shape=[
            jax.ShapeDtypeStruct((first, inner, cells), f32),
            jax.ShapeDtypeStruct((first // 2, inner // 2, third), f32),
        ],
        scratch_shapes=[pltpu.VMEM((2, 2, tall, cells), f32)] * 3
        + [pltpu.VMEM((3, rows, cells), f32)] * 2
        + [
            pltpu.VMEM((3, 2, rows, cells), f32),
            pltpu.VMEM((3, 2, tall, cells), f32),
            pltpu.VMEM((3, 2, rows, cells), f32),
        ],
        compiler_params=pltpu.CompilerParams(dimension_semantics=("arbitrary",)),
    )(grown, widened, *tables)


def body(spectrum, scalar):
    groups_x = lax.axis_size("px")
    groups_y = lax.axis_size("py")
    spec_second = spectrum.shape[2]
    spec_third = spectrum.shape[3]
    length_first = spectrum.shape[4]
    length_second = spec_second * groups_x
    length_third = spec_third * groups_y
    cells_first = length_first // groups_x
    cells_second = length_second // groups_y
    factor = 1.0 / math.sqrt(length_first * length_second * length_third)
    wave_first = wavenumbers(length_first)
    third_local = lax.dynamic_slice_in_dim(
        wavenumbers(length_third), lax.axis_index("py") * spec_third, spec_third
    )
    real_part = spectrum[0]
    imag_part = spectrum[1]
    first_cos, first_sin = dft_table(length_first, 1.0)
    line_wave = wave_first[None, None, None, :]
    real_fields = jnp.concatenate([real_part, -line_wave * imag_part[1:]])
    imag_fields = jnp.concatenate([imag_part, line_wave * real_part[1:]])
    real_lines = jnp.transpose(real_fields, (1, 0, 2, 3)).reshape(
        spec_second, 5 * spec_third, length_first
    )
    imag_lines = jnp.transpose(imag_fields, (1, 0, 2, 3)).reshape(
        spec_second, 5 * spec_third, length_first
    )
    out_real, out_imag = complex_apply(real_lines, imag_lines, first_cos, first_sin, "qlk,kx->qxl")
    landed = across_px(jnp.stack([out_real, out_imag]))
    wave_second = wavenumbers(length_second)[:, None, None]
    wave_third = third_local[None, None, :]
    real_in = landed[0]
    imag_in = landed[1]

    def member(array, index):
        return array[..., index * spec_third : (index + 1) * spec_third]

    omega_real = [
        -(wave_second * member(imag_in, 2) - wave_third * member(imag_in, 1)),
        -wave_third * member(imag_in, 0) - member(real_in, 4),
        member(real_in, 3) + wave_second * member(imag_in, 0),
    ]
    omega_imag = [
        wave_second * member(real_in, 2) - wave_third * member(real_in, 1),
        wave_third * member(real_in, 0) - member(imag_in, 4),
        member(imag_in, 3) - wave_second * member(real_in, 0),
    ]
    arrived = jnp.stack(
        [
            jnp.concatenate([real_in[..., : 3 * spec_third]] + omega_real, axis=-1),
            jnp.concatenate([imag_in[..., : 3 * spec_third]] + omega_imag, axis=-1),
        ]
    )
    second_cos, second_sin = dft_table(length_second, 1.0)
    out_real, out_imag = complex_apply(
        arrived[0], arrived[1], second_cos, second_sin, "pxl,py->yxl"
    )
    arrived = across_py(jnp.stack([out_real, out_imag])[:, None])
    ordered = arrived.reshape(2, groups_y, cells_second, cells_first, 6, spec_third)
    ordered = jnp.transpose(ordered, (0, 4, 3, 2, 1, 5)).reshape(
        2, 6, cells_first, cells_second, length_third
    )
    third_cos, third_sin = dft_table(length_third, 1.0)
    physical = (
        contract("cxyn,nz->cxyz", ordered[0], third_cos)
        - contract("cxyn,nz->cxyz", ordered[1], third_sin)
    ) * factor
    velocity = physical[:3]
    vorticity = physical[3:]
    widened = padded(velocity, (("px", 1, 4), ("py", 2, 4)))
    grown = padded(scalar, (("px", 0, 6), ("py", 1, ROW_PAD)))
    theta, buoyancy = scalar_steps(grown, widened)
    forcing = jnp.stack(
        [
            velocity[1] * vorticity[2] - velocity[2] * vorticity[1],
            velocity[2] * vorticity[0] - velocity[0] * vorticity[2],
            velocity[0] * vorticity[1] - velocity[1] * vorticity[0] + buoyancy,
        ]
    )
    back_cos, back_sin = dft_table(length_third, -1.0)
    force_lines = forcing.reshape(3 * cells_first * cells_second, length_third)
    sectioned = jnp.stack(
        [contract("lz,zn->nl", force_lines, back_cos), contract("lz,zn->nl", force_lines, back_sin)]
    )
    arrived = across_py(sectioned[:, None])
    ordered = arrived.reshape(2, groups_y, spec_third, 3, cells_first, cells_second)
    ordered = jnp.transpose(ordered, (0, 2, 3, 4, 1, 5)).reshape(
        2, spec_third * 3 * cells_first, length_second
    )
    back_cos, back_sin = dft_table(length_second, -1.0)
    out_real, out_imag = complex_apply(ordered[0], ordered[1], back_cos, back_sin, "ly,yp->pl")
    arrived = across_px(jnp.stack([out_real, out_imag])[:, None])
    ordered = arrived.reshape(2, groups_x, spec_second, spec_third, 3, cells_first)
    ordered = jnp.transpose(ordered, (0, 4, 2, 3, 1, 5)).reshape(
        2, 3, spec_second, spec_third, length_first
    )
    back_cos, back_sin = dft_table(length_first, -1.0)
    out_real, out_imag = complex_apply(ordered[0], ordered[1], back_cos, back_sin, "cqsx,xk->cqsk")
    tendency = jnp.stack([out_real, out_imag]) * factor
    return (tendency, theta)


def solution(mesh):
    in_specs = (P(None, None, "px", "py", None), P("px", "py", None))
    out_specs = (P(None, None, "px", "py", None), P("px", "py", None))
    return jax.shard_map(body, mesh=mesh, in_specs=in_specs, out_specs=out_specs, check_vma=False)
```

```python
import math

import jax
import jax.numpy as jnp
from jax import lax
from jax.experimental import pallas as pl
from jax.experimental.pallas import tpu as pltpu
from jax.sharding import PartitionSpec as P

NSUB = 3


STEP_RATIO = 0.08
DIFFUSION_RATIO = 1.0


def padded(block, sides):
    for axis, dim, width in sides:
        count = lax.axis_size(axis)
        forward = [(i, i + 1) for i in range(count - 1)]
        forward.append((count - 1, 0))
        backward = [(target, source) for source, target in forward]
        low = lax.ppermute(
            lax.slice_in_dim(block, block.shape[dim] - width, None, axis=dim), axis, forward
        )
        high = lax.ppermute(lax.slice_in_dim(block, 0, width, axis=dim), axis, backward)
        block = jnp.concatenate([low, block, high], axis=dim)
    return block


def contract(form, left, right):
    return jnp.einsum(form, left, right, precision=lax.Precision.HIGH)


def dft_table(length, sign):
    index = jnp.arange(length, dtype=jnp.int32)
    product = index[:, None] * index[None, :] % length
    angle = 2.0 * math.pi / length * product.astype(jnp.float32)
    return (jnp.cos(angle), sign * jnp.sin(angle))


def complex_apply(real, imag, cosine, sine, form):
    return (
        contract(form, real, cosine) - contract(form, imag, sine),
        contract(form, real, sine) + contract(form, imag, cosine),
    )


def upsample_table(length):
    rows = jnp.arange(length, dtype=jnp.int32)[:, None]
    cols = jnp.arange(2 * length, dtype=jnp.int32)[None, :]
    half = cols // 2
    is_odd = cols % 2 == 1
    near = jnp.logical_or(rows == half, rows == (half + 1) % length)
    distant = jnp.logical_or(rows == (half - 1) % length, rows == (half + 2) % length)
    even_part = jnp.where(jnp.logical_and(jnp.logical_not(is_odd), rows == half), 1.0, 0.0)
    odd_part = jnp.where(
        is_odd, jnp.where(near, 9.0 / 16.0, 0.0) - jnp.where(distant, 1.0 / 16.0, 0.0), 0.0
    )
    return (even_part + odd_part).astype(jnp.float32)


def pair_table(length):
    rows = jnp.arange(2 * length, dtype=jnp.int32)[:, None]
    cols = jnp.arange(length, dtype=jnp.int32)[None, :]
    return jnp.where(rows // 2 == cols, 0.125, 0.0).astype(jnp.float32)


def wavenumbers(length):
    index = jnp.arange(length, dtype=jnp.int32)
    signed = jnp.where(index < length // 2, index, index - length)
    return 2.0 * math.pi / length * signed.astype(jnp.float32)


def across_px(pieces):
    return lax.all_to_all(pieces, "px", split_axis=0, concat_axis=0, tiled=True)


ROW_PAD = 8


def refine_rows(points):
    rows = jnp.arange(2 * points, dtype=jnp.int32)[:, None]
    cols = jnp.arange(points, dtype=jnp.int32)[None, :]

    def weights(row):
        half = row // 2
        gap = cols - half
        near = jnp.logical_or(gap == 0, gap == 1)
        distant = jnp.logical_or(gap == -1, gap == 2)
        odd = jnp.where(near, 9.0 / 16.0, 0.0) - jnp.where(distant, 1.0 / 16.0, 0.0)
        return jnp.where(row % 2 == 1, odd, jnp.where(gap == 0, 1.0, 0.0))

    cell = weights(rows)
    return cell, 0.5 * (cell + weights(rows + 1))


def split(value):
    high = value.astype(jnp.bfloat16)
    return high, (value - high.astype(jnp.float32)).astype(jnp.bfloat16)


def table_right(value, table):
    high, low = split(value)
    return jnp.dot(high, table, preferred_element_type=jnp.float32) + jnp.dot(
        low, table, preferred_element_type=jnp.float32
    )


def table_left(table, value):
    high, low = split(value)
    return jnp.dot(table, high, preferred_element_type=jnp.float32) + jnp.dot(
        table, low, preferred_element_type=jnp.float32
    )


def half_slope(first, second):
    low = jnp.minimum(first, second)
    high = jnp.maximum(first, second)
    return 0.5 * (jnp.maximum(low, 0.0) + jnp.minimum(high, 0.0))


def upwind(face, left, right, jump):
    return face * jnp.where(face > 0.0, left, right) - DIFFUSION_RATIO * jump


def line_div(theta, face, axis):
    size = theta.shape[axis]
    jump = pltpu.roll(theta, size - 1, axis) - theta
    slope = half_slope(pltpu.roll(jump, 1, axis), jump)
    right = pltpu.roll(theta - slope, size - 1, axis)
    flux = upwind(face, theta + slope, right, jump)
    return flux - pltpu.roll(flux, 1, axis)


def substep(prev, new, slope_ref, flux_ref, fx, fy, fz, store, first, count, chunk):
    def run(index, carry):
        row = pl.multiple_of(first + index * chunk, 8)
        here = pl.ds(row, chunk)
        inner = pl.ds(pl.multiple_of(row + ROW_PAD, 8), chunk)
        wide = pl.ds(row, chunk + 2 * ROW_PAD)
        b0 = prev[0, inner]
        b1 = prev[1, inner]
        a0 = new[0, inner]
        a1 = new[1, inner]
        jump_b = b1 - b0
        jump_m = a0 - b1
        slope_b = half_slope(jump_b, jump_m)
        slope_a = half_slope(jump_m, a1 - a0)
        flux_0 = upwind(fx[0, here], b0 + slope_ref[here], b1 - slope_b, jump_b)
        flux_1 = upwind(fx[1, here], b1 + slope_b, a0 - slope_a, jump_m)
        div_0 = flux_0 - flux_ref[here]
        div_1 = flux_1 - flux_0
        slope_ref[here] = slope_a
        flux_ref[here] = flux_1
        for plane, (base, div) in enumerate(((b0, div_0), (b1, div_1))):
            side = line_div(prev[plane, wide], fy[plane, wide], 0)
            side = side[ROW_PAD : ROW_PAD + chunk]
            total = div + side + line_div(base, fz[plane, here], 1)
            store(plane, row, base - STEP_RATIO * total)
        return carry

    lax.fori_loop(0, count, run, 0)


def march(
    theta_ref, speed_ref, my_ref, myf_ref, mz_ref, mzf_ref, py_ref, pz_ref,
    out_ref, pool_ref, t0, t1, t2, slopes, fluxes, fx, fy, fz,
):
    step = pl.program_id(0)
    now = lax.rem(step, 2)
    old = 1 - now
    rows = theta_ref.shape[1]
    inner = pl.ds(ROW_PAD, rows)
    t0[now, 0, inner] = theta_ref[0]
    t0[now, 1, inner] = theta_ref[1]
    slot = lax.rem(step, 3)
    before = lax.rem(step + 2, 3)
    oldest = lax.rem(step + 1, 3)
    for part in range(3):
        q0 = speed_ref[part, step]
        q1 = speed_ref[part, step + 1]
        qm = speed_ref[part, jnp.maximum(step - 1, 0)]
        q2 = speed_ref[part, step + 2]
        odd = (9.0 * (q0 + q1) - (qm + q2)) * (1.0 / 16.0)
        pair = (0.5 * (q0 + odd), 0.5 * (odd + q1)) if part == 0 else (q0, odd)
        for plane in range(2):
            line = table_right(pair[plane], (mzf_ref if part == 2 else mz_ref)[...])
            full = table_left((myf_ref if part == 1 else my_ref)[...], line)
            if part == 1:
                fy[slot, plane, inner] = full
            else:
                (fx if part == 0 else fz)[slot, plane] = full
    whole = rows // 24 if rows % 24 == 0 else rows // 8
    chunk = rows // whole

    def keep(target):
        def store(plane, row, value):
            target[now, plane, pl.ds(pl.multiple_of(row + ROW_PAD, 8), value.shape[0])] = value

        return store

    def emit(plane, row, value):
        out_ref[plane, pl.ds(pl.multiple_of(row - ROW_PAD, 8), value.shape[0])] = value

    substep(
        t0.at[old], t0.at[now], slopes.at[0], fluxes.at[0],
        fx.at[slot], fy.at[slot], fz.at[slot], keep(t1), 0, whole, chunk,
    )
    substep(
        t1.at[old], t1.at[now], slopes.at[1], fluxes.at[1],
        fx.at[before], fy.at[before], fz.at[before], keep(t2), 0, whole, chunk,
    )
    last = rows - 2 * ROW_PAD
    last_chunk = 32 if last % 32 == 0 else 8
    substep(
        t2.at[old], t2.at[now], slopes.at[2], fluxes.at[2],
        fx.at[oldest], fy.at[oldest], fz.at[oldest], emit, ROW_PAD, last // last_chunk, last_chunk,
    )
    both = out_ref[0] + out_ref[1]
    pool_ref[0] = table_left(py_ref[...], table_right(both, pz_ref[...]))


def scalar_steps(grown, widened):
    planes, rows, cells = grown.shape
    wide_first, wide_second, third = widened.shape[1:]
    steps = planes // 2
    first = planes - 12
    inner = rows - 2 * ROW_PAD
    cell, face = refine_rows(wide_second)
    up = upsample_table(third)
    up_face = 0.5 * (up + jnp.roll(up, -1, axis=1))
    pool_rows = (8.0 * pair_table(inner // 2)).T
    tables = [cell, face, up, up_face, pool_rows, pair_table(third)]
    tables = [table.astype(jnp.bfloat16) for table in tables]
    tall = rows + 2 * ROW_PAD
    f32 = jnp.float32
    return pl.pallas_call(
        march,
        grid=(steps,),
        in_specs=[
            pl.BlockSpec((2, rows, cells), lambda g: (g, 0, 0)),
            pl.BlockSpec((3, wide_first, wide_second, third), lambda g: (0, 0, 0, 0)),
        ]
        + [pl.BlockSpec(table.shape, lambda g: (0, 0)) for table in tables],
        out_specs=[
            pl.BlockSpec((2, inner, cells), lambda g: (jnp.maximum(g - 6, 0), 0, 0)),
            pl.BlockSpec((1, inner // 2, third), lambda g: (jnp.maximum(g - 6, 0), 0, 0)),
        ],
        out_shape=[
            jax.ShapeDtypeStruct((first, inner, cells), f32),
            jax.ShapeDtypeStruct((first // 2, inner // 2, third), f32),
        ],
        scratch_shapes=[pltpu.VMEM((2, 2, tall, cells), f32)] * 3
        + [pltpu.VMEM((3, rows, cells), f32)] * 2
        + [
            pltpu.VMEM((3, 2, rows, cells), f32),
            pltpu.VMEM((3, 2, tall, cells), f32),
            pltpu.VMEM((3, 2, rows, cells), f32),
        ],
        compiler_params=pltpu.CompilerParams(dimension_semantics=("arbitrary",)),
        cost_estimate=pl.CostEstimate(
            flops=400 * NSUB * grown.size, bytes_accessed=400 * grown.size, transcendentals=0
        ),
    )(grown, widened, *tables)


def split_table(table):
    high = lax.reduce_precision(table, exponent_bits=8, mantissa_bits=7)
    return jnp.stack([high, table - high]).astype(jnp.bfloat16)


def product(left, right):
    total = jnp.dot(left[0], right[1], preferred_element_type=jnp.float32)
    total += jnp.dot(left[1], right[0], preferred_element_type=jnp.float32)
    return total + jnp.dot(left[0], right[0], preferred_element_type=jnp.float32)


def to_physical(lines_ref, second_ref, third_ref, left_ref, right_ref, out_ref):
    span = third_ref.shape[1]
    k2 = second_ref[...]
    k3 = third_ref[...]
    groups, _, lines, part, _ = out_ref.shape
    left = (left_ref[0], left_ref[1])
    right = (right_ref[0], right_ref[1])
    length = left_ref.shape[1] // 2
    for x in range(lines):
        real = lines_ref[0, :, x, :]
        imag = lines_ref[1, :, x, :]
        re = [real[:, i * span : (i + 1) * span] for i in range(5)]
        im = [imag[:, i * span : (i + 1) * span] for i in range(5)]
        omega_re = [
            -(k2 * im[2] - k3 * im[1]),
            -k3 * im[0] - re[4],
            re[3] + k2 * im[0],
        ]
        omega_im = [
            k2 * re[2] - k3 * re[1],
            k3 * re[0] - im[4],
            im[3] - k2 * re[0],
        ]
        whole = jnp.concatenate(
            [
                jnp.concatenate(re[:3] + omega_re, axis=1),
                jnp.concatenate(im[:3] + omega_im, axis=1),
            ],
            axis=0,
        )
        turned = product(left, split(whole))
        for field in range(6):
            cut = slice(field * span, (field + 1) * span)
            line = jnp.concatenate([turned[:length, cut], turned[length:, cut]], axis=1)
            value = product(split(line), right)
            for group in range(groups):
                out_ref[group, field, x] = value[group * part : (group + 1) * part]


def physical_parts(landed, wave_second, wave_third, groups, length_third, factor):
    _, length_second, lines, wide = landed.shape
    span = wave_third.shape[0]
    block = 8
    cos2, sin2 = dft_table(length_second, 1.0)
    left = jnp.concatenate(
        [jnp.concatenate([cos2, -sin2], axis=1), jnp.concatenate([sin2, cos2], axis=1)]
    )
    start = lax.axis_index("py") * span
    cos3, sin3 = dft_table(length_third, 1.0)
    right = factor * jnp.concatenate(
        [
            lax.dynamic_slice_in_dim(cos3, start, span),
            -lax.dynamic_slice_in_dim(sin3, start, span),
        ]
    )
    part = length_second // groups
    return pl.pallas_call(
        to_physical,
        grid=(lines // block,),
        in_specs=[
            pl.BlockSpec((2, length_second, block, wide), lambda g: (0, 0, g, 0)),
            pl.BlockSpec((length_second, 1), lambda g: (0, 0)),
            pl.BlockSpec((1, span), lambda g: (0, 0)),
            pl.BlockSpec((2,) + left.shape, lambda g: (0, 0, 0)),
            pl.BlockSpec((2,) + right.shape, lambda g: (0, 0, 0)),
        ],
        out_specs=pl.BlockSpec(
            (groups, 6, block, part, length_third), lambda g: (0, 0, g, 0, 0)
        ),
        out_shape=jax.ShapeDtypeStruct((groups, 6, lines, part, length_third), jnp.float32),
        compiler_params=pltpu.CompilerParams(dimension_semantics=("arbitrary",)),
    )(landed, wave_second[:, None], wave_third[None, :], split_table(left), split_table(right))


def back_second(force_ref, table_ref, out_ref):
    groups, fields, lines, _, both = force_ref.shape
    span = both // 2
    owners, _, _, rows, _ = out_ref.shape
    table = (table_ref[0], table_ref[1])
    length = table_ref.shape[1] // 2

    def run(x, carry):
        data = jnp.concatenate(
            [
                jnp.concatenate([force_ref[g, f, x] for g in range(groups)], axis=0)
                for f in range(fields)
            ],
            axis=1,
        )
        turned = product(table, split(data))
        for f in range(fields):
            top = turned[:length, f * both : (f + 1) * both]
            low = turned[length:, f * both : (f + 1) * both]
            value = jnp.concatenate(
                [top[:, :span] - low[:, span:], low[:, :span] + top[:, span:]], axis=1
            )
            for owner in range(owners):
                out_ref[owner, x, f] = value[owner * rows : (owner + 1) * rows]
        return carry

    lax.fori_loop(0, lines, run, 0)


def second_lines(arrived, owners):
    groups, fields, lines, part, both = arrived.shape
    length = groups * part
    rows = length // owners
    block = 8
    cosine, sine = dft_table(length, -1.0)
    table = split_table(jnp.concatenate([cosine, sine]))
    return pl.pallas_call(
        back_second,
        grid=(lines // block,),
        in_specs=[
            pl.BlockSpec((groups, fields, block, part, both), lambda g: (0, 0, g, 0, 0)),
            pl.BlockSpec(table.shape, lambda g: (0, 0, 0)),
        ],
        out_specs=pl.BlockSpec((owners, block, fields, rows, both), lambda g: (0, g, 0, 0, 0)),
        out_shape=jax.ShapeDtypeStruct((owners, lines, fields, rows, both), jnp.float32),
        compiler_params=pltpu.CompilerParams(dimension_semantics=("arbitrary",)),
    )(arrived, table)


def back_first(early_ref, late_ref, table_ref, out_ref):
    owners, lines, _, rows, both = early_ref.shape
    span = both // 2
    length = owners * lines
    early = pl.num_programs(0) - 1

    def run(data_ref):
        table = (table_ref[0], table_ref[1])
        for q in range(rows):
            data = data_ref[:, :, 0, q, :].reshape(length, both)
            turned = product(split(data.T), table)
            out_ref[0, 0, q] = turned[:span, :length] - turned[span:, length:]
            out_ref[1, 0, q] = turned[:span, length:] + turned[span:, :length]

    @pl.when(pl.program_id(0) < early)
    def _():
        run(early_ref)

    @pl.when(pl.program_id(0) == early)
    def _():
        run(late_ref)


def first_lines(early, late, factor):
    owners, lines, fields, rows, both = early.shape
    length = owners * lines
    cosine, sine = dft_table(length, -1.0)
    table = split_table(factor * jnp.concatenate([cosine, sine], axis=1))
    block = (owners, lines, 1, rows, both)
    return pl.pallas_call(
        back_first,
        grid=(fields + 1,),
        in_specs=[
            pl.BlockSpec(block, lambda f: (0, 0, jnp.minimum(f, fields - 1), 0, 0)),
            pl.BlockSpec(block, lambda f: (0, 0, 0, 0, 0)),
            pl.BlockSpec(table.shape, lambda f: (0, 0, 0)),
        ],
        out_specs=pl.BlockSpec((2, 1, rows, both // 2, length), lambda f: (0, f, 0, 0, 0)),
        out_shape=jax.ShapeDtypeStruct((2, fields + 1, rows, both // 2, length), jnp.float32),
        compiler_params=pltpu.CompilerParams(dimension_semantics=("arbitrary",)),
    )(early, late, table)


def body(spectrum, scalar):
    groups_x = lax.axis_size("px")
    groups_y = lax.axis_size("py")
    spec_second = spectrum.shape[2]
    spec_third = spectrum.shape[3]
    length_first = spectrum.shape[4]
    length_second = spec_second * groups_x
    length_third = spec_third * groups_y
    factor = 1.0 / math.sqrt(length_first * length_second * length_third)
    wave_first = wavenumbers(length_first)
    third_local = lax.dynamic_slice_in_dim(
        wavenumbers(length_third), lax.axis_index("py") * spec_third, spec_third
    )
    real_part = spectrum[0]
    imag_part = spectrum[1]
    first_cos, first_sin = dft_table(length_first, 1.0)
    line_wave = wave_first[None, None, None, :]
    real_fields = jnp.concatenate([real_part, -line_wave * imag_part[1:]])
    imag_fields = jnp.concatenate([imag_part, line_wave * real_part[1:]])
    real_lines = jnp.transpose(real_fields, (1, 0, 2, 3)).reshape(
        spec_second, 5 * spec_third, length_first
    )
    imag_lines = jnp.transpose(imag_fields, (1, 0, 2, 3)).reshape(
        spec_second, 5 * spec_third, length_first
    )
    out_real, out_imag = complex_apply(real_lines, imag_lines, first_cos, first_sin, "qlk,kx->qxl")
    landed = lax.all_to_all(
        jnp.stack([out_real, out_imag]), "px", split_axis=2, concat_axis=1, tiled=True
    )
    parts = physical_parts(
        landed, wavenumbers(length_second), third_local, groups_y, length_third, factor
    )
    physical = lax.all_to_all(parts, "py", split_axis=0, concat_axis=0, tiled=True).sum(axis=0)
    velocity = physical[:3]
    vorticity = physical[3:]
    back_cos, back_sin = dft_table(length_third, -1.0)

    def send_back(force):
        pieces = []
        for group in range(groups_y):
            cut = slice(group * spec_third, (group + 1) * spec_third)
            table = jnp.concatenate([back_cos[:, cut], back_sin[:, cut]], axis=1)
            pieces.append(contract("cxyz,zn->cxyn", force, table))
        arrived = lax.all_to_all(jnp.stack(pieces), "py", split_axis=0, concat_axis=0, tiled=True)
        return second_lines(arrived, groups_x)

    early = send_back(
        jnp.stack(
            [
                velocity[1] * vorticity[2] - velocity[2] * vorticity[1],
                velocity[2] * vorticity[0] - velocity[0] * vorticity[2],
            ]
        )
    )
    widened = padded(velocity, (("px", 1, 4), ("py", 2, 4)))
    grown = padded(scalar, (("px", 0, 6), ("py", 1, ROW_PAD)))
    widened, early = lax.optimization_barrier((widened, early))
    early = across_px(early)
    theta, buoyancy = scalar_steps(grown, widened)
    early, buoyancy = lax.optimization_barrier((early, buoyancy))
    late = send_back(
        (velocity[0] * vorticity[1] - velocity[1] * vorticity[0] + buoyancy)[None]
    )
    late = across_px(late)
    tendency = first_lines(early, late, factor)
    return (tendency, theta)


def solution(mesh):
    in_specs = (P(None, None, "px", "py", None), P("px", "py", None))
    out_specs = (P(None, None, "px", "py", None), P("px", "py", None))
    return jax.shard_map(
        body, mesh=mesh, in_specs=in_specs, out_specs=out_specs, check_vma=False
    )
```
